32 devices in a mesh: sec: 8 (over z, y), tile: 4 (over x, core).
Axes of the slice: x: 2, y: 2, z: 4, core: 2. Of those that a mesh axis runs over, the one named last changes fastest.
Arguments:
- images: bfloat16 [16, 128, 256], P('sec', 'tile'), may hold values from -6 to 6
- seam_links: int32 [16, 3], replicated, may hold values 0 or 1
- partners: int32 [16, 3], P('sec'), may hold values from 0 to 15, as said below
- enc_first: bfloat16 [64, 1, 3, 3], replicated, may hold values from -3 to 3
- enc_second: bfloat16 [64, 64, 3, 3], replicated, may hold values from -0.375 to 0.375
- enc_third: bfloat16 [32, 64, 1, 1], replicated, may hold values from -1 to 1
- dec_first: bfloat16 [64, 81, 3, 3], replicated, may hold values from -0.3125 to 0.3125
- dec_second: bfloat16 [64, 64, 3, 3], replicated, may hold values from -0.375 to 0.375
- dec_third: bfloat16 [2, 64, 3, 3], replicated, may hold values from -0.375 to 0.375
Outputs:
- descriptors: bfloat16 [16, 32, 64, 128], P('sec', None, 'tile')
- flows: float32 [16, 3, 2, 64, 128], P('sec', None, None, 'tile')
The draws below stay inside these ranges and needn't reach their ends.
Inputs may be any that keep to these rules, and one draw needn't show every extreme that they name: partners[s, j] is s + o or s - o, with o = 1, 2, 4 for j = 0, 1, 2.
All inputs are finite; a program needn't handle non-finite values.
Results may differ from the reference program's by a relative error of at most 0.0098.
Values may be sent and summed in bfloat16 or wider, within the bound.
No kernel may reach another device: no remote copies, remote signals or barrier semaphores. Data moves between devices by JAX's collectives and lax.ppermute only.
A program may use at most 128 MiB of HBM per device.

```python
import math
import jax
import jax.numpy as jnp
from jax import lax

TILE_H = 32
TILE_W = 256
ENC_CH = 64
DESC = 32
DEC_CH = 64
RADIUS = 4
DISP = 81
SECTIONS = 16
IMG_H = 128
N_TILE = 4


def draw_partners(key, part):
    section_ids = jnp.arange(SECTIONS, dtype=jnp.int32)
    columns = []
    for slot_index, offset in enumerate((1, 2, 4)):
        coin_flips = jax.random.randint(jax.random.fold_in(key, 17 + slot_index), (SECTIONS,), 0, 2)
        forward_flag = jnp.where(section_ids == SECTIONS - 1 - offset, 1, jnp.where(section_ids == offset, 0, coin_flips))
        forward_flag = jnp.where(section_ids < offset, 1, jnp.where(section_ids >= SECTIONS - offset, 0, forward_flag))
        columns.append(jnp.where(forward_flag == 1, section_ids + offset, section_ids - offset))
    return jnp.stack(columns, axis=1).astype(jnp.int32)


def set_ends(entries, own_key, low, largest):
    longest = entries.shape.index(max(entries.shape))
    spots = []
    for shift in (0, 1):
        where = [jax.random.randint(jax.random.fold_in(own_key, axis), (), 0, length) for axis, length in enumerate(entries.shape)]
        where[longest] = (where[longest] + shift) % entries.shape[longest]
        spots.append(tuple(where))
    return entries.at[spots[0]].set(low).at[spots[1]].set(largest)


def shard_levels(key, extent, shards, least, high):
    loudness, own = 1.0, jax.random.fold_in(key, 6)
    for dim, parts in shards:
        draws = jnp.exp(jax.random.uniform(jax.random.fold_in(own, dim), (parts,), jnp.float32, least / len(shards), high / len(shards)))
        loudness = loudness * jnp.repeat(draws, extent[dim] // parts).reshape([-1 if axis == dim else 1 for axis in range(len(extent))])
    return loudness


def centred(key, dims, scale, bound, cuts=(), kind=jnp.bfloat16):
    gain = shard_levels(key, dims, cuts, -0.22, 0.18) if cuts else 1.0
    values = jax.random.normal(key, dims, jnp.float32) * scale * gain
    return jnp.minimum(jnp.maximum(values, -bound), bound).astype(kind)


def setup_inputs(seed: int = 0) -> dict:
    streams_of = jax.random.split(jax.random.key(seed), 10)
    images = centred(streams_of[0], (SECTIONS, IMG_H, TILE_W), 1.0, 6.0, ((0, 8), (1, 4)))
    seam_links = set_ends((jax.random.randint(streams_of[1], (SECTIONS, N_TILE - 1), 0, 8) < 7).astype(jnp.int32), jax.random.fold_in(streams_of[1], 1), 0, 1)
    partners = draw_partners(jax.random.fold_in(streams_of[9], 71), 0)
    enc_first = centred(streams_of[3], (ENC_CH, 1, 3, 3), 4 ** -0.5, 3.0)
    enc_second = centred(streams_of[4], (ENC_CH, ENC_CH, 3, 3), (ENC_CH * 9 // 2) ** -0.5, 0.375)
    enc_third = centred(streams_of[5], (DESC, ENC_CH, 1, 1), (ENC_CH // 2) ** -0.5, 1.0)
    dec_first = centred(streams_of[6], (DEC_CH, DISP, 3, 3), (DISP * 9 // 2) ** -0.5, 0.3125)
    dec_second = centred(streams_of[7], (DEC_CH, DEC_CH, 3, 3), (DEC_CH * 9 // 2) ** -0.5, 0.375)
    dec_third = centred(streams_of[8], (2, DEC_CH, 3, 3), (DEC_CH * 9 // 2) ** -0.5, 0.375)
    return {"images": images, "seam_links": seam_links, "partners": partners, "enc_first": enc_first, "enc_second": enc_second, "enc_third": enc_third, "dec_first": dec_first, "dec_second": dec_second, "dec_third": dec_third}


leak_slope = 0.1

def leaky_relu(values):
    return jnp.maximum(values, leak_slope * values)

def convolve(values, kernel, stride, dilation):
    width_pad = dilation * (kernel.shape[3] // 2)
    return lax.conv_general_dilated(values.astype(jnp.float32), kernel.astype(jnp.float32), (stride, stride), ((0, 0), (width_pad, width_pad)), rhs_dilation=(dilation, dilation), dimension_numbers=('NCHW', 'OIHW', 'NCHW'), precision=lax.Precision.HIGHEST)

def link_pair(links_row):
    linked = links_row.astype(jnp.float32)
    nothing = jnp.zeros((1,), jnp.float32)
    return (jnp.concatenate([nothing, linked]), jnp.concatenate([linked, nothing]))

def extend(values, margin, lower_link, upper_link):
    blank_rows = jnp.zeros_like(values[:1, ..., :margin, :])
    below_rows = jnp.concatenate([blank_rows, values[:-1, ..., values.shape[-2] - margin:, :]], axis=0)
    above_rows = jnp.concatenate([values[1:, ..., :margin, :], blank_rows], axis=0)
    target_shape = (-1,) + (1,) * (values.ndim - 1)
    below_rows = below_rows * lower_link.reshape(target_shape).astype(values.dtype)
    above_rows = above_rows * upper_link.reshape(target_shape).astype(values.dtype)
    return jnp.concatenate([below_rows, values, above_rows], axis=-2)

def encode(section_image, links_row, encoder_weights):
    first_kernel, second_kernel, third_kernel = encoder_weights
    lower_link, upper_link = link_pair(links_row)
    tile_rows = section_image.reshape(N_TILE, TILE_H, TILE_W)
    blank_rows = jnp.zeros_like(tile_rows[:1, -1:, :])
    edge_rows = jnp.concatenate([blank_rows, tile_rows[:-1, -1:, :]], axis=0)
    edge_rows = edge_rows * lower_link[:, None, None].astype(tile_rows.dtype)
    stacked = jnp.concatenate([edge_rows, tile_rows], axis=1)[:, None]
    first_maps = leaky_relu(convolve(stacked, first_kernel, 2, 1)).astype(jnp.bfloat16)
    widened = extend(first_maps, 2, lower_link, upper_link)
    second_maps = leaky_relu(convolve(widened, second_kernel, 1, 2)).astype(jnp.bfloat16)
    return convolve(second_maps, third_kernel, 1, 1).astype(jnp.bfloat16)

def correlate(own_desc, partner_desc):
    window_span = 2 * RADIUS + 1
    height = own_desc.shape[2]
    breadth = own_desc.shape[3]
    padded_rows = jnp.pad(partner_desc, ((0, 0), (0, 0), (0, 0), (RADIUS, RADIUS)))
    own_wide = own_desc.astype(jnp.float32)
    terms = [lax.optimization_barrier(jnp.sum(own_wide * padded_rows[:, :, row_shift:row_shift + height, col_shift:col_shift + breadth].astype(jnp.float32), axis=1)) for row_shift in range(window_span) for col_shift in range(window_span)]
    return (jnp.stack(terms, axis=1) / math.sqrt(DESC)).astype(jnp.bfloat16)

def decode(cost_volume, lower_link, upper_link, decoder_weights):
    hidden = cost_volume
    for layer_index, kernel in enumerate(decoder_weights):
        result = convolve(extend(hidden, 1, lower_link, upper_link), kernel, 1, 1)
        if layer_index < len(decoder_weights) - 1:
            hidden = leaky_relu(result).astype(jnp.bfloat16)
        else:
            hidden = result
    return hidden

def reference(images, seam_links, partners, enc_first, enc_second, enc_third, dec_first, dec_second, dec_third):
    encoder_weights = (enc_first, enc_second, enc_third)
    decoder_weights = (dec_first, dec_second, dec_third)

    def encode_section(inputs):
        return encode(inputs[0], inputs[1], encoder_weights)
    all_desc = lax.map(encode_section, (images, seam_links))

    def decode_section(section):
        own_desc = all_desc[section]
        lower_link, upper_link = link_pair(seam_links[section])
        flow_list = []
        for slot_index in range(3):
            target = partners[section, slot_index]
            partner_lower, partner_upper = link_pair(seam_links[target])
            partner_desc = extend(all_desc[target], RADIUS, partner_lower, partner_upper)
            cost_volume = correlate(own_desc, partner_desc)
            flow_list.append(decode(cost_volume, lower_link, upper_link, decoder_weights))
        return jnp.stack(flow_list)
    flows = lax.map(decode_section, jnp.arange(SECTIONS, dtype=jnp.int32))
    descriptors = all_desc.transpose(0, 2, 1, 3, 4).reshape(SECTIONS, DESC, IMG_H // 2, TILE_W // 2)
    flows = flows.transpose(0, 1, 3, 2, 4, 5).reshape(SECTIONS, 3, 2, IMG_H // 2, TILE_W // 2)
    return (descriptors, flows)
```

```python
import functools
import math

import jax
import jax.numpy as jnp
from jax import lax
from jax.experimental import pallas as pl
from jax.experimental.pallas import tpu as pltpu
from jax.sharding import PartitionSpec as P

RADIUS = 4
WINDOW = 2 * RADIUS + 1
SLOPE = 0.1
OFFSETS = (1, 2, 4)

f32 = jnp.float32
bf16 = jnp.bfloat16


def dot(a, b):
    return jnp.dot(a, b, preferred_element_type=f32)


def leaky(v):
    return jnp.maximum(v, SLOPE * v)


def iota(shape, dim):
    return lax.broadcasted_iota(jnp.int32, shape, dim)


def col_shift(v, by):
    width = v.shape[-1]
    rolled = pltpu.roll(v, (-by) % width, axis=v.ndim - 1)
    x = iota(v.shape, v.ndim - 1) + by
    return jnp.where((x >= 0) & (x < width), rolled, 0.0)


def stack_cols(v, by):
    return jnp.concatenate(
        [col_shift(v, -by).astype(bf16), v.astype(bf16), col_shift(v, by).astype(bf16)], axis=0
    )


def onehot(shape, cond):
    return jnp.where(cond, 1.0, 0.0).astype(bf16)


def body(
    meta_ref, links_ref, partners_ref, img_ref, ha_ref, hb_ref,
    w1_ref, w2_ref, w3_ref, d1_ref, d2_ref, d3_ref,
    desc_ref, flow_ref,
    ext, sel, w1t, w2c, d1c, d2c, d3c, dmap, own, cost,
):
    here = img_ref.shape[0] // 6
    n_seam = links_ref.shape[1]
    sec = meta_ref[0]
    tile = meta_ref[1]
    desc_ch = w3_ref.shape[0]
    enc_ch = w3_ref.shape[1]
    width = desc_ref.shape[3]
    in_width = img_ref.shape[2]

    r = iota((in_width, 3 * width), 0)
    q = iota((in_width, 3 * width), 1)
    sel[...] = onehot(None, r == 2 * (q % width) + q // width - 1)
    j = iota((9, 8 * 128), 0)
    lane = iota((9, 8 * 128), 1)
    m, kx, ql = lane // 128, (lane % 128) // 32, lane % 32
    place = onehot(None, (j % 3 == kx) & (ql == 2 * m + j // 3))
    spread = lax.dot_general(
        w1_ref[...], place, (((0,), (0,)), ((), ())), preferred_element_type=f32
    ).astype(bf16)
    for i in range(8):
        w1t[enc_ch * i : enc_ch * (i + 1), :] = spread[:, 128 * i : 128 * (i + 1)]
    disp = d1_ref.shape[2]
    main = disp - 1
    r = iota((disp, 256), 0)
    q = iota((disp, 256), 1)
    for ky in range(3):
        acc = jnp.zeros((enc_ch, 256), f32)
        for kx in range(3):
            put = onehot(None, ((r < main) & (q == kx * main + r)) | ((r == main) & (q == 3 * main + kx)))
            acc = acc + dot(d1_ref[3 * ky + kx], put)
        d1c[enc_ch * ky : enc_ch * (ky + 1), :] = acc.astype(bf16)
        r2 = iota((enc_ch, 3 * enc_ch), 0)
        q2 = iota((enc_ch, 3 * enc_ch), 1)
        for src, dst, pitch in ((w2_ref, w2c, enc_ch), (d2_ref, d2c, enc_ch), (d3_ref, d3c, 8)):
            rows = src.shape[1]
            acc = jnp.zeros((rows, 3 * enc_ch), f32)
            for kx in range(3):
                acc = acc + dot(src[3 * ky + kx], onehot(None, q2 == kx * enc_ch + r2))
            dst[pitch * ky : pitch * ky + rows, :] = acc.astype(dst.dtype)
    cost[...] = jnp.zeros_like(cost)

    def link(section, seam):
        inside = (seam >= 0) & (seam < n_seam)
        value = links_ref[section, jnp.clip(seam, 0, n_seam - 1)]
        return jnp.where(inside, value, 0).astype(f32)

    def encode(cand, low, up):
        height = img_ref.shape[1]

        @pl.when(tile % 2 == 0)
        def _():
            ext[0:height, :] = hb_ref[cand]
            ext[2 * height : 3 * height, :] = ha_ref[cand]

        @pl.when(tile % 2 == 1)
        def _():
            ext[0:height, :] = ha_ref[cand]
            ext[2 * height : 3 * height, :] = hb_ref[cand]

        ext[height : 2 * height, :] = img_ref[cand]
        taps = dot(ext[...], sel[...]).astype(bf16)
        down = onehot(None, iota((112, 96), 0) == iota((112, 96), 1) + 1)
        taps = dot(down, taps).astype(bf16)
        blank = jnp.zeros((32, width), bf16)

        def window(first, factor=None):
            parts = []
            for kx in range(3):
                part = taps[first : first + 32, kx * width : (kx + 1) * width]
                if factor is not None:
                    scale = jnp.where(iota((32, width), 0) == 0, factor, 1.0)
                    part = (part.astype(f32) * scale).astype(bf16)
                parts.append(part)
            return jnp.concatenate(parts + [blank], axis=0)

        feats = {}

        def keep(out, first, lane0):
            for i in range(out.shape[0] // enc_ch):
                v = leaky(out[enc_ch * i : enc_ch * (i + 1), lane0 : lane0 + width])
                feats[first + i] = stack_cols(v, 2)

        keep(dot(w1t[6 * enc_ch :, :], window(0)), -10, 0)
        pair = dot(w1t[...], jnp.concatenate([window(16), window(32, low)], axis=1))
        keep(pair, -8, 0)
        keep(pair, 0, width)
        pair = dot(w1t[...], jnp.concatenate([window(48), window(64, up)], axis=1))
        keep(pair, 8, 0)
        keep(pair, 16, width)
        keep(dot(w1t[: 2 * enc_ch, :], window(80)), 24, 0)

        parts = {}
        for p in range(-5, 13):
            x = jnp.concatenate([feats[2 * p], feats[2 * p + 1]], axis=1)
            if p == -5:
                parts[p] = (dot(w2c[:enc_ch, :], x), None, None)
            elif p == 12:
                parts[p] = (None, None, dot(w2c[2 * enc_ch :, :], x))
            else:
                t = dot(w2c[...], x)
                parts[p] = (t[:enc_ch], t[enc_ch : 2 * enc_ch], t[2 * enc_ch :])
            o = p - 1
            if o < -4:
                continue
            before, mid, after = parts[o - 1][0], parts[o][1], parts[o + 1][2]
            if o == 0:
                before = before * low
            if o == 8:
                before = before * up
            if o == -1:
                after = after * low
            if o == 7:
                after = after * up
            second = leaky(before + mid + after).astype(bf16)
            d = dot(w3_ref[...], second).astype(bf16).astype(f32)
            for half in range(2):
                row = 2 * o + half + 8
                dmap[pl.ds(row, desc_ch, stride=32), :] = d[:, half * width : (half + 1) * width]

    def correlate(low_p, up_p, low_s, up_s):
        for k in range(3):
            y = iota((8, width), 0) + (8 * k - RADIUS)
            self_mask = jnp.where(y < 0, low_s, jnp.where(y >= 16, up_s, 1.0)) * (
                1.0 / math.sqrt(desc_ch)
            )
            for g in range(3):
                init = tuple(jnp.zeros((8, width), f32) for _ in range(27))

                def step(c, acc, k=k, g=g):
                    acc = list(acc)
                    mine = [
                        own[3 * g + b, pl.ds(pl.multiple_of(c * 24, 8) + 8 * k, 8), :]
                        for b in range(3)
                    ]
                    for a in range(9):
                        other = dmap[pl.ds(c * 32 + 8 * k + a, 8), :]
                        for b in range(3):
                            acc[3 * a + b] = acc[3 * a + b] + mine[b] * other
                    return tuple(acc)

                acc = lax.fori_loop(0, desc_ch, step, init, unroll=4)
                for a in range(9):
                    yp = y + (a - RADIUS)
                    mask = self_mask
                    if k == 0:
                        mask = jnp.where((y < 0) != (yp < 0), mask * low_p, mask)
                    if k == 2:
                        mask = jnp.where((y < 16) != (yp < 16), mask * up_p, mask)
                    for b in range(3):
                        by = 3 * g + b - RADIUS
                        v = col_shift(acc[3 * a + b] * mask, by)
                        d = a * WINDOW + 3 * g + b
                        if d < WINDOW * WINDOW - 1:
                            cost[pl.ds(8 * k * 96 + d, 8, stride=96), :] = v
                        else:
                            for i, s in enumerate((-1, 0, 1)):
                                moved = v if s == 0 else col_shift(v, s)
                                cost[pl.ds(8 * k * 96 + d + i, 8, stride=96), :] = moved

    def decode(sec_i, slot, low_s, up_s):
        def rows_of(t, pitch, base):
            pass

        t1 = {}
        for p in range(-2, 10):
            halves = []
            for row in (2 * p, 2 * p + 1):
                at = (row + RADIUS) * 96
                v = cost[at : at + 96, :]
                v80 = v[:80].astype(bf16).astype(f32)
                halves.append(
                    jnp.concatenate([stack_cols(v80, 1), v[80:96].astype(bf16)], axis=0)
                )
            t = dot(d1c[...], jnp.concatenate(halves, axis=1))
            t1[2 * p] = t[:, :width]
            t1[2 * p + 1] = t[:, width:]

        def join(t, row, pitch, n):
            return (
                t[row - 1][:n] + t[row][pitch : pitch + n] + t[row + 1][2 * pitch : 2 * pitch + n]
            )

        def hidden(t, row):
            v = leaky(join(t, row, enc_ch, enc_ch))
            if row < 0:
                v = v * low_s
            if row >= 16:
                v = v * up_s
            return stack_cols(v, 1)

        t2 = {}
        for p in range(-1, 9):
            x = jnp.concatenate([hidden(t1, 2 * p), hidden(t1, 2 * p + 1)], axis=1)
            t = dot(d2c[...], x)
            t2[2 * p] = t[:, :width]
            t2[2 * p + 1] = t[:, width:]
        t3 = {}
        for p in range(9):
            x = jnp.concatenate([hidden(t2, 2 * p - 1), hidden(t2, 2 * p)], axis=1)
            t = dot(d3c[...].astype(bf16), x)
            t3[2 * p - 1] = t[:, :width]
            t3[2 * p] = t[:, width:]
        for row in range(16):
            v = join(t3, row, 8, 2)
            for o in range(2):
                flow_ref[sec_i, slot, o, row : row + 1, :] = v[o : o + 1, :]

    def section(sec_i, carry):
        mine = sec * here + sec_i
        low_s = link(mine, tile - 1)
        up_s = link(mine, tile)
        encode(sec_i, low_s, up_s)

        def keep_own(c, carry):
            v = dmap[pl.ds(c * 32 + RADIUS, 24), :]
            at = pl.multiple_of(c * 24, 8)
            for b in range(WINDOW):
                by = (b - RADIUS) % width
                own[b, pl.ds(at, 24), :] = pltpu.roll(v, by, axis=1) if by else v
            desc_ref[sec_i, c] = v[RADIUS : RADIUS + 16].astype(bf16)
            return carry

        lax.fori_loop(0, desc_ch, keep_own, 0)

        def pair(slot, carry):
            other = partners_ref[sec_i, slot]
            dev = other // here
            away = (dev // 2) - (sec // 2)
            near_a = (dev // 2) == ((sec // 2) ^ 1)
            block = jnp.where(away == 0, 0, jnp.where(near_a, 1, 2))
            twin = jnp.where(dev % 2 == sec % 2, 0, 1)
            cand = (block * 2 + twin) * here + other % here
            low_p = link(other, tile - 1)
            up_p = link(other, tile)
            encode(cand, low_p, up_p)
            correlate(low_p, up_p, low_s, up_s)
            decode(sec_i, slot, low_s, up_s)
            return carry

        return lax.fori_loop(0, len(OFFSETS), pair, carry)

    lax.fori_loop(0, here, section, 0)


def swap(x, axis, first, stride=1):
    size = lax.axis_size(axis)
    route = []
    for i in range(first * stride, size - stride):
        if (i // stride - first) % 2 == 0:
            route += [(i, i + stride), (i + stride, i)]
    return lax.ppermute(x, axis, route)


def shards(
    images, seam_links, partners, enc_first, enc_second, enc_third, dec_first, dec_second, dec_third
):
    here, height, in_width = images.shape
    assert here * 2 >= max(OFFSETS) and lax.axis_size("sec") % 2 == 0
    meta = jnp.stack([lax.axis_index("sec"), lax.axis_index("tile")]).astype(jnp.int32)
    near = jnp.concatenate([images, swap(images, "sec", 0)], axis=0)
    cands = jnp.concatenate([near, swap(near, "sec", 0, 2), swap(near, "sec", 1, 2)], axis=0)
    ha = swap(cands, "tile", 0)
    hb = swap(cands, "tile", 1)

    def taps(w):
        return jnp.transpose(w, (2, 3, 0, 1)).reshape((-1,) + w.shape[:2])

    w1 = jnp.transpose(enc_first, (1, 2, 3, 0)).reshape(9, -1)
    w3 = enc_third[:, :, 0, 0]
    enc_ch = enc_first.shape[0]
    desc_ch = enc_third.shape[0]
    rows, width = height // 2, in_width // 2
    smem = pl.BlockSpec(memory_space=pltpu.SMEM)
    vmem = pl.BlockSpec(memory_space=pltpu.VMEM)
    return pl.pallas_call(
        body,
        in_specs=[smem] * 3 + [vmem] * 9,
        out_specs=[vmem] * 2,
        out_shape=[
            jax.ShapeDtypeStruct((here, desc_ch, rows, width), bf16),
            jax.ShapeDtypeStruct((here, len(OFFSETS), dec_third.shape[0], rows, width), f32),
        ],
        scratch_shapes=[
            pltpu.VMEM((3 * height, in_width), bf16),
            pltpu.VMEM((in_width, 3 * width), bf16),
            pltpu.VMEM((8 * enc_ch, 128), bf16),
            pltpu.VMEM((3 * enc_ch, 3 * enc_ch), bf16),
            pltpu.VMEM((3 * enc_ch, 256), bf16),
            pltpu.VMEM((3 * enc_ch, 3 * enc_ch), bf16),
            pltpu.VMEM((24, 3 * enc_ch), f32),
            pltpu.VMEM((desc_ch * 32, width), f32),
            pltpu.VMEM((WINDOW, desc_ch * 24, width), f32),
            pltpu.VMEM((24 * 96, width), f32),
        ],
        compiler_params=pltpu.CompilerParams(vmem_limit_bytes=48 * 1024 * 1024),
    )(meta, seam_links, partners, cands, ha, hb, w1, taps(enc_second), w3, taps(dec_first),
      taps(dec_second), taps(dec_third))


def solution(mesh):
    return jax.shard_map(
        shards,
        mesh=mesh,
        in_specs=(P("sec", "tile", None), P(), P("sec", None), P(), P(), P(), P(), P(), P()),
        out_specs=(P("sec", None, "tile", None), P("sec", None, None, "tile", None)),
        check_vma=False,
    )
```

```python
import functools
import math

import jax
import jax.numpy as jnp
from jax import lax
from jax.experimental import pallas as pl
from jax.experimental.pallas import tpu as pltpu
from jax.sharding import PartitionSpec as P

RADIUS = 4
WINDOW = 2 * RADIUS + 1
SLOPE = 0.1
LAG = 3
OFFSETS = (1, 2, 4)

f32 = jnp.float32
bf16 = jnp.bfloat16


def dot(a, b):
    return jnp.dot(a, b, preferred_element_type=f32)


def leaky(v):
    return jnp.maximum(v, SLOPE * v)


def iota(shape, dim):
    return lax.broadcasted_iota(jnp.int32, shape, dim)


def col_shift(v, by):
    width = v.shape[-1]
    rolled = pltpu.roll(v, (-by) % width, axis=v.ndim - 1)
    x = iota(v.shape, v.ndim - 1) + by
    return jnp.where((x >= 0) & (x < width), rolled, jnp.zeros_like(rolled))


def stack_cols(v, by):
    v = v.astype(bf16)
    return jnp.concatenate([col_shift(v, -by), v, col_shift(v, by)], axis=0)


def onehot(shape, cond):
    return jnp.where(cond, 1.0, 0.0).astype(bf16)


def body(
    meta_ref, links_ref, partners_ref, img_ref, ha_ref, hb_ref,
    w1_ref, w2_ref, w3_ref, d1_ref, d2_ref, d3_ref,
    desc_ref, flow_ref,
    sel, w1t, w2c, d1c, d2c, d3c, dmap_a, dmap_b, own, ownh, win, winh, cost_a, cost_b,
):
    here = img_ref.shape[0] // 6
    n_seam = links_ref.shape[1]
    sec = meta_ref[0]
    tile = meta_ref[1]
    desc_ch = w3_ref.shape[0]
    enc_ch = w3_ref.shape[1]
    width = desc_ref.shape[3]
    in_width = img_ref.shape[2]

    r = iota((in_width, 3 * width), 0)
    q = iota((in_width, 3 * width), 1)
    sel[...] = onehot(None, r == 2 * (q % width) + q // width - 1)
    j = iota((9, 8 * 128), 0)
    lane = iota((9, 8 * 128), 1)
    m, kx, ql = lane // 128, (lane % 128) // 32, lane % 32
    place = onehot(None, (j % 3 == kx) & (ql == 2 * m + j // 3))
    spread = lax.dot_general(
        w1_ref[...], place, (((0,), (0,)), ((), ())), preferred_element_type=f32
    ).astype(bf16)
    for i in range(8):
        w1t[enc_ch * i : enc_ch * (i + 1), :] = spread[:, 128 * i : 128 * (i + 1)]
    disp = d1_ref.shape[2]
    main = disp - 1
    r = iota((disp, 256), 0)
    q = iota((disp, 256), 1)
    for ky in range(3):
        acc = jnp.zeros((enc_ch, 256), f32)
        for kx in range(3):
            put = onehot(None, ((r < main) & (q == kx * main + r)) | ((r == main) & (q == 3 * main + kx)))
            acc = acc + dot(d1_ref[3 * ky + kx], put)
        d1c[enc_ch * ky : enc_ch * (ky + 1), :] = acc.astype(bf16)
        r2 = iota((enc_ch, 3 * enc_ch), 0)
        q2 = iota((enc_ch, 3 * enc_ch), 1)
        for src, dst, pitch in ((w2_ref, w2c, enc_ch), (d2_ref, d2c, enc_ch), (d3_ref, d3c, 8)):
            rows = src.shape[1]
            acc = jnp.zeros((rows, 3 * enc_ch), f32)
            for kx in range(3):
                acc = acc + dot(src[3 * ky + kx], onehot(None, q2 == kx * enc_ch + r2))
            dst[pitch * ky : pitch * ky + rows, :] = acc.astype(dst.dtype)
    for cost in (cost_a, cost_b):
        cost[...] = jnp.zeros_like(cost)
    even = tile % 2 == 0
    one = jnp.where(tile >= 0, 1.0, 0.0).astype(f32)
    pace = {}
    one_row = (jnp.zeros((16, width), f32) + one).astype(bf16)

    def paced(v, by=None):
        tick = pace.get("tick")
        if tick is None:
            return v * (one if by is None else by)
        factor = tick if by is None else tick * by
        return (v.reshape(-1, 8, width) * factor[None]).reshape(v.shape)


    def link(section, seam):
        inside = (seam >= 0) & (seam < n_seam)
        value = links_ref[section, jnp.clip(seam, 0, n_seam - 1)]
        return jnp.where(inside, value, 0).astype(f32)

    def encode(dmap, cand, low, up):
        taps, feats, parts = [], {}, {}
        blank = jnp.zeros((32, width), bf16)

        def start():
            first, second = ha_ref[cand], hb_ref[cand]
            strip = [jnp.where(even, second, first), img_ref[cand], jnp.where(even, first, second)]
            cols = dot(jnp.concatenate(strip, axis=0), sel[...]).astype(bf16)
            down = onehot(None, iota((112, 96), 0) == iota((112, 96), 1) + 1)
            taps.append(dot(down, cols).astype(bf16))

        def window(first, factor=None):
            rows = []
            for kx in range(3):
                part = taps[0][first : first + 32, kx * width : (kx + 1) * width]
                if "tick" in pace and kx == 0:
                    part = paced(part.astype(f32)).astype(bf16)
                if factor is not None:
                    scale = jnp.where(iota((32, width), 0) == 0, factor, 1.0)
                    part = (part.astype(f32) * scale).astype(bf16)
                rows.append(part)
            return jnp.concatenate(rows + [blank], axis=0)

        def conv_first(first_row, lhs, *rhs):
            out = dot(w1t[lhs, :], jnp.concatenate([window(*w) for w in rhs], axis=1))
            for i in range(out.shape[0] // enc_ch):
                for j in range(len(rhs)):
                    feats[first_row + 8 * j + i] = out[
                        enc_ch * i : enc_ch * (i + 1), width * j : width * (j + 1)
                    ]

        def activate(r):
            v = feats[r]
            feats[r] = stack_cols(jnp.maximum(v, paced(v, SLOPE)), 2)

        def conv_second(p):
            x = jnp.concatenate([feats[2 * p], feats[2 * p + 1]], axis=1)
            if p == -5:
                parts[p] = (dot(w2c[:enc_ch, :], x), None, None)
            elif p == 12:
                parts[p] = (None, None, dot(w2c[2 * enc_ch :, :], x))
            else:
                t = dot(w2c[...], x)
                parts[p] = (t[:enc_ch], t[enc_ch : 2 * enc_ch], t[2 * enc_ch :])

        def wide(v, by):
            return jnp.concatenate([paced(v[:, :width], by), paced(v[:, width:], by)], axis=1)

        def project(o):
            before, mid, after = parts[o - 1][0], parts[o][1], parts[o + 1][2]
            before = wide(before, {0: low, 8: up}.get(o))
            after = wide(after, {-1: low, 7: up}.get(o))
            second = leaky(before + mid + after).astype(bf16)
            d = dot(w3_ref[...], second).astype(bf16).astype(f32)
            for half in range(2):
                row = 2 * o + half + 8
                dmap[pl.ds(row, desc_ch, stride=33), :] = d[:, half * width : (half + 1) * width]

        part = functools.partial
        steps = [start, part(conv_first, -10, slice(6 * enc_ch, None), (0,))]
        steps += [part(conv_first, -8 + i, slice(i * enc_ch, (i + 2) * enc_ch), (16,), (32, low)) for i in range(0, 8, 2)]
        steps += [part(conv_first, 8 + i, slice(i * enc_ch, (i + 2) * enc_ch), (48,), (64, up)) for i in range(0, 8, 2)]
        steps += [part(conv_first, 24, slice(0, 2 * enc_ch), (80,))]
        steps += [part(activate, r) for r in range(-10, 26)]
        for p in range(-5, 13):
            steps.append(part(conv_second, p))
            if p - LAG >= -4:
                steps.append(part(project, p - LAG))
        steps += [part(project, p) for p in range(13 - LAG, 12)]
        return steps

    def windows(dmap, c):
        top = iota((8, width), 0) < RADIUS
        for a in range(WINDOW):
            at = c * 33 + a
            win[a, c] = dmap[pl.ds(at + RADIUS, 16), :].astype(bf16)
            rim = jnp.where(top, dmap[pl.ds(at, 8), :], dmap[pl.ds(at + 16, 8), :])
            winh[a, c] = jnp.concatenate([rim, rim], axis=0).astype(bf16)

    def both(u, v):
        uv = jnp.concatenate([u, v], axis=0)
        return uv[: u.shape[0]], uv[u.shape[0] :]

    def accumulate(state, n, left, right, c):
        mine = [both(left(i, c), left(i, c + 1)) for i in range(n)]
        mine = [[m * one_row for m in pair] for pair in mine]
        fresh = c % 8 == 0
        part = [None] * (WINDOW * n) if fresh else state["part"]
        for a in range(WINDOW):
            other = both(right(a, c), right(a, c + 1))
            for i in range(n):
                at = a * n + i
                v = mine[i][0] * other[0]
                part[at] = v if fresh else part[at] + v
                part[at] = part[at] + mine[i][1] * other[1]
        state["part"] = part
        if c % 8 == 6:
            pace["tick"] = part[0][:8].astype(f32) * (1.0 - one) + one
        if c % 8 == 6:
            total = state.get("total")
            state["total"] = part if total is None else [p + q for p, q in zip(total, part)]

    def put(cost, v, by, d, row):
        v = col_shift(v, by)
        last = WINDOW * WINDOW - 1
        for i, s in ((0, 0),) if d < last else ((0, -1), (1, 0), (2, 1)):
            moved = v if s == 0 else col_shift(v, s)
            cost[pl.ds(row * 97 + d + i, 8, stride=97), :] = moved

    def correlate(dmap, cost, sec_i, low_p, up_p, low_s, up_s):
        scale = 1.0 / math.sqrt(desc_ch)
        y = iota((8, width), 0)

        def tile_rows(state, b0, n, a):
            for i in range(n):
                v = state["total"][a * n + i].astype(f32) * scale
                by = b0 + i - RADIUS
                d = a * WINDOW + b0 + i
                first, second = v[:8], v[8:]
                if a < RADIUS:
                    first = jnp.where(y + (a - RADIUS) < 0, first * low_p, first)
                if a > RADIUS:
                    second = jnp.where(y + (8 + a - RADIUS) >= 16, second * up_p, second)
                put(cost, first, by, d, RADIUS)
                put(cost, second, by, d, RADIUS + 8)

        def halo_rows(state, q0, n, a):
            yh = jnp.where(y < RADIUS, y - RADIUS, y + 12)
            side = jnp.where(y < RADIUS, low_s, up_s) * scale
            torn = jnp.where(y < RADIUS, low_p, up_p)
            yp = yh + (a - RADIUS)
            mask = jnp.where((yp >= 0) & (yp < 16), side * torn, side)
            for i in range(n):
                v = state["total"][a * n + i].astype(f32)
                for h in range(2):
                    b = 2 * (q0 + i) + h
                    if b < WINDOW:
                        puth(cost, v[8 * h : 8 * h + 8] * mask, b - RADIUS, a * WINDOW + b)

        part = functools.partial
        steps = [part(windows, dmap, c) for c in range(desc_ch)]
        for b0 in range(0, WINDOW, 2):
            n = min(2, WINDOW - b0)
            state = {}

            def left(i, c, b0=b0):
                return own[sec_i, b0 + i, c]

            def right(a, c):
                return win[a, c]

            steps += [part(accumulate, state, n, left, right, c) for c in range(0, desc_ch, 2)]
            steps += [part(tile_rows, state, b0, n, a) for a in range(WINDOW)]
        for q0 in range(0, (WINDOW + 1) // 2, 2):
            n = min(2, (WINDOW + 1) // 2 - q0)
            state = {}

            def left(i, c, q0=q0):
                return ownh[sec_i, q0 + i, c]

            def right(a, c):
                return winh[a, c]

            steps += [part(accumulate, state, n, left, right, c) for c in range(0, desc_ch, 2)]
            steps += [part(halo_rows, state, q0, n, a) for a in range(WINDOW)]
        return steps

    def puth(cost, v, by, d):
        v = col_shift(v, by)
        last = WINDOW * WINDOW - 1
        for i, s in ((0, 0),) if d < last else ((0, -1), (1, 0), (2, 1)):
            moved = v if s == 0 else col_shift(v, s)
            cost[pl.ds(d + i, RADIUS, stride=97), :] = moved[:RADIUS]
            cost[pl.ds((RADIUS + 16) * 97 + d + i, RADIUS, stride=97), :] = moved[RADIUS:]

    def decode(cost, sec_i, slot, low_s, up_s):
        t1, t2, t3 = {}, {}, {}

        def cost_row(row):
            at = (row + RADIUS) * 97
            v = paced(cost[at : at + 96, :]).astype(bf16)
            return jnp.concatenate([stack_cols(v[:80], 1), v[80:]], axis=0)

        def join(t, row, pitch, n):
            before, after = t[row - 1][:n], t[row + 1][2 * pitch : 2 * pitch + n]
            if n % 8:
                return before * one + t[row][pitch : pitch + n] + after * one
            return paced(before) + t[row][pitch : pitch + n] + paced(after)

        def hidden(t, row):
            v = leaky(join(t, row, enc_ch, enc_ch))
            if row < 0:
                v = v * low_s
            if row >= 16:
                v = v * up_s
            return stack_cols(v, 1)

        def multiply(t, weights, row, rows):
            out = dot(weights, jnp.concatenate(rows, axis=1))
            t[row], t[row + 1] = out[:, :width], out[:, width:]

        def first(p):
            multiply(t1, d1c[...], 2 * p, [cost_row(2 * p), cost_row(2 * p + 1)])

        def second(p):
            multiply(t2, d2c[...], 2 * p, [hidden(t1, 2 * p), hidden(t1, 2 * p + 1)])

        def third(p):
            rows = [hidden(t2, 2 * p - 1), hidden(t2, 2 * p)]
            multiply(t3, d3c[...].astype(bf16), 2 * p - 1, rows)
            for row in (2 * p - 2, 2 * p - 1):
                if 0 <= row < 16:
                    v = join(t3, row, 8, 2)
                    for o in range(2):
                        flow_ref[sec_i, slot, o, row : row + 1, :] = v[o : o + 1, :]

        part = functools.partial
        return (
            [part(first, p) for p in range(-2, 10)]
            + [part(second, p) for p in range(-1, 9)]
            + [part(third, p) for p in range(9)]
        )

    def run(*lists):
        keyed = [
            ((k + 0.5) / len(steps), n, k, f) for n, steps in enumerate(lists) for k, f in enumerate(steps)
        ]
        pace.clear()
        for _, _, _, f in sorted(keyed, key=lambda e: e[:3]):
            f()
        pace.clear()

    def section(sec_i, carry):
        mine = sec * here + sec_i
        run(encode(dmap_a, sec_i, link(mine, tile - 1), link(mine, tile)))

        def keep_own(c, carry):
            tile_rows = dmap_a[pl.ds(c * 33 + 8, 16), :].astype(bf16)
            top = iota((8, width), 0) < RADIUS
            rim = jnp.where(top, dmap_a[pl.ds(c * 33 + 4, 8), :], dmap_a[pl.ds(c * 33 + 20, 8), :])
            desc_ref[sec_i, c] = tile_rows

            def moved(v, b):
                by = (b - RADIUS) % width
                return pltpu.roll(v, by, axis=1) if by else v

            for b in range(WINDOW):
                own[sec_i, b, c] = moved(tile_rows, b)
            for h in range((WINDOW + 1) // 2):
                pair_rows = [moved(rim, 2 * h), moved(rim, min(2 * h + 1, WINDOW - 1))]
                ownh[sec_i, h, c] = jnp.concatenate(pair_rows, axis=0).astype(bf16)
            return carry

        return lax.fori_loop(0, desc_ch, keep_own, carry, unroll=4)

    lax.fori_loop(0, here, section, 0)

    n_slot = len(OFFSETS)
    n_pair = here * n_slot

    def pair_of(i):
        i = jnp.clip(i, 0, n_pair - 1)
        sec_i, slot = i // n_slot, i % n_slot
        mine = sec * here + sec_i
        other = partners_ref[sec_i, slot]
        dev = other // here
        near_a = (dev // 2) == ((sec // 2) ^ 1)
        block = jnp.where(dev // 2 == sec // 2, 0, jnp.where(near_a, 1, 2))
        twin = jnp.where(dev % 2 == sec % 2, 0, 1)
        cand = (block * 2 + twin) * here + other % here
        links = (link(other, tile - 1), link(other, tile), link(mine, tile - 1), link(mine, tile))
        return sec_i, slot, cand, links

    def encode_pair(i, dmap):
        _, _, cand, links = pair_of(i)
        return encode(dmap, cand, links[0], links[1])

    def decode_pair(i, cost):
        sec_i, slot, _, links = pair_of(i)
        return decode(cost, sec_i, slot, links[2], links[3])

    def phase(i, dmap, next_dmap, cost, last_cost):
        sec_i, _, _, links = pair_of(i)
        run(
            correlate(dmap, cost, sec_i, *links),
            decode_pair(i - 1, last_cost) + encode_pair(i + 1, next_dmap),
        )

    run(encode_pair(0, dmap_a))

    def two(k, carry):
        phase(2 * k, dmap_a, dmap_b, cost_a, cost_b)
        phase(2 * k + 1, dmap_b, dmap_a, cost_b, cost_a)
        return carry

    assert n_pair % 2 == 0
    lax.fori_loop(0, n_pair // 2, two, 0)
    run(decode_pair(n_pair - 1, cost_b))


def swap(x, axis, first, stride=1):
    size = lax.axis_size(axis)
    route = []
    for i in range(first * stride, size - stride):
        if (i // stride - first) % 2 == 0:
            route += [(i, i + stride), (i + stride, i)]
    return lax.ppermute(x, axis, route)


def shards(
    images, seam_links, partners, enc_first, enc_second, enc_third, dec_first, dec_second, dec_third
):
    here, height, in_width = images.shape
    assert here * 2 >= max(OFFSETS) and lax.axis_size("sec") % 2 == 0
    meta = jnp.stack([lax.axis_index("sec"), lax.axis_index("tile")]).astype(jnp.int32)
    near = jnp.concatenate([images, swap(images, "sec", 0)], axis=0)
    cands = jnp.concatenate([near, swap(near, "sec", 0, 2), swap(near, "sec", 1, 2)], axis=0)
    ha = swap(cands, "tile", 0)
    hb = swap(cands, "tile", 1)

    def taps(w):
        return jnp.transpose(w, (2, 3, 0, 1)).reshape((-1,) + w.shape[:2])

    w1 = jnp.transpose(enc_first, (1, 2, 3, 0)).reshape(9, -1)
    w3 = enc_third[:, :, 0, 0]
    enc_ch = enc_first.shape[0]
    desc_ch = enc_third.shape[0]
    rows, width = height // 2, in_width // 2
    smem = pl.BlockSpec(memory_space=pltpu.SMEM)
    vmem = pl.BlockSpec(memory_space=pltpu.VMEM)
    return pl.pallas_call(
        body,
        in_specs=[smem] * 3 + [vmem] * 9,
        out_specs=[vmem] * 2,
        out_shape=[
            jax.ShapeDtypeStruct((here, desc_ch, rows, width), bf16),
            jax.ShapeDtypeStruct((here, len(OFFSETS), dec_third.shape[0], rows, width), f32),
        ],
        scratch_shapes=[
            pltpu.VMEM((in_width, 3 * width), bf16),
            pltpu.VMEM((8 * enc_ch, 128), bf16),
            pltpu.VMEM((3 * enc_ch, 3 * enc_ch), bf16),
            pltpu.VMEM((3 * enc_ch, 256), bf16),
            pltpu.VMEM((3 * enc_ch, 3 * enc_ch), bf16),
            pltpu.VMEM((24, 3 * enc_ch), f32),
            pltpu.VMEM((desc_ch * 33, width), f32),
            pltpu.VMEM((desc_ch * 33, width), f32),
            pltpu.VMEM((here, WINDOW, desc_ch, rows, width), bf16),
            pltpu.VMEM((here, (WINDOW + 1) // 2, desc_ch, rows, width), bf16),
            pltpu.VMEM((WINDOW, desc_ch, rows, width), bf16),
            pltpu.VMEM((WINDOW, desc_ch, rows, width), bf16),
            pltpu.VMEM((24 * 97, width), f32),
            pltpu.VMEM((24 * 97, width), f32),
        ],
        compiler_params=pltpu.CompilerParams(vmem_limit_bytes=48 * 1024 * 1024),
    )(meta, seam_links, partners, cands, ha, hb, w1, taps(enc_second), w3, taps(dec_first),
      taps(dec_second), taps(dec_third))


def solution(mesh):
    return jax.shard_map(
        shards,
        mesh=mesh,
        in_specs=(P("sec", "tile", None), P(), P("sec", None), P(), P(), P(), P(), P(), P()),
        out_specs=(P("sec", None, "tile", None), P("sec", None, None, "tile", None)),
        check_vma=False,
    )
```

```python
import functools
import math

import jax
import jax.numpy as jnp
from jax import lax
from jax.experimental import pallas as pl
from jax.experimental.pallas import tpu as pltpu
from jax.sharding import PartitionSpec as P

RADIUS = 4
WINDOW = 2 * RADIUS + 1
SLOPE = 0.1
LAG = 3
OFFSETS = (1, 2, 4)

f32 = jnp.float32
bf16 = jnp.bfloat16


def dot(a, b):
    return jnp.dot(a, b, preferred_element_type=f32)


def leaky(v):
    return jnp.maximum(v, SLOPE * v)


def iota(shape, dim):
    return lax.broadcasted_iota(jnp.int32, shape, dim)


def col_shift(v, by):
    width = v.shape[-1]
    rolled = pltpu.roll(v, (-by) % width, axis=v.ndim - 1)
    x = iota(v.shape, v.ndim - 1) + by
    return jnp.where((x >= 0) & (x < width), rolled, jnp.zeros_like(rolled))


def stack_cols(v, by):
    v = v.astype(bf16)
    return jnp.concatenate([col_shift(v, -by), v, col_shift(v, by)], axis=0)


def onehot(shape, cond):
    return jnp.where(cond, 1.0, 0.0).astype(bf16)


def body(
    meta_ref, links_ref, partners_ref, img_ref, ha_ref, hb_ref,
    w1_ref, w2_ref, w3_ref, d1_ref, d2_ref, d3_ref,
    desc_ref, flow_ref,
    sel, w1t, w2c, d1c, d2c, d3c, dmap_a, dmap_b, own, cost_a, cost_b,
):
    here = img_ref.shape[0] // 6
    n_seam = links_ref.shape[1]
    sec = meta_ref[0]
    tile = meta_ref[1]
    desc_ch = w3_ref.shape[0]
    enc_ch = w3_ref.shape[1]
    width = desc_ref.shape[3]
    in_width = img_ref.shape[2]

    r = iota((in_width, 3 * width), 0)
    q = iota((in_width, 3 * width), 1)
    sel[...] = onehot(None, r == 2 * (q % width) + q // width - 1)
    j = iota((9, 8 * 128), 0)
    lane = iota((9, 8 * 128), 1)
    m, kx, ql = lane // 128, (lane % 128) // 32, lane % 32
    place = onehot(None, (j % 3 == kx) & (ql == 2 * m + j // 3))
    spread = lax.dot_general(
        w1_ref[...], place, (((0,), (0,)), ((), ())), preferred_element_type=f32
    ).astype(bf16)
    for i in range(8):
        w1t[enc_ch * i : enc_ch * (i + 1), :] = spread[:, 128 * i : 128 * (i + 1)]
    disp = d1_ref.shape[2]
    main = disp - 1
    r = iota((disp, 256), 0)
    q = iota((disp, 256), 1)
    for ky in range(3):
        acc = jnp.zeros((enc_ch, 256), f32)
        for kx in range(3):
            put = onehot(None, ((r < main) & (q == kx * main + r)) | ((r == main) & (q == 3 * main + kx)))
            acc = acc + dot(d1_ref[3 * ky + kx], put)
        d1c[enc_ch * ky : enc_ch * (ky + 1), :] = acc.astype(bf16)
        r2 = iota((enc_ch, 3 * enc_ch), 0)
        q2 = iota((enc_ch, 3 * enc_ch), 1)
        for src, dst, pitch in ((w2_ref, w2c, enc_ch), (d2_ref, d2c, enc_ch), (d3_ref, d3c, 8)):
            rows = src.shape[1]
            acc = jnp.zeros((rows, 3 * enc_ch), f32)
            for kx in range(3):
                acc = acc + dot(src[3 * ky + kx], onehot(None, q2 == kx * enc_ch + r2))
            dst[pitch * ky : pitch * ky + rows, :] = acc.astype(dst.dtype)
    for cost in (cost_a, cost_b):
        cost[...] = jnp.zeros_like(cost)
    even = tile % 2 == 0
    one = jnp.where(tile >= 0, 1.0, 0.0).astype(f32)
    pace = {}

    def paced(v, by=None):
        tick = pace.get("tick")
        if tick is None:
            return v * (one if by is None else by)
        factor = tick if by is None else tick * by
        return (v.reshape(-1, 8, width) * factor[None]).reshape(v.shape)


    def link(section, seam):
        inside = (seam >= 0) & (seam < n_seam)
        value = links_ref[section, jnp.clip(seam, 0, n_seam - 1)]
        return jnp.where(inside, value, 0).astype(f32)

    def encode(dmap, cand, low, up):
        taps, feats, parts = [], {}, {}
        blank = jnp.zeros((32, width), bf16)

        def start():
            first, second = ha_ref[cand], hb_ref[cand]
            strip = [jnp.where(even, second, first), img_ref[cand], jnp.where(even, first, second)]
            cols = dot(jnp.concatenate(strip, axis=0), sel[...]).astype(bf16)
            down = onehot(None, iota((112, 96), 0) == iota((112, 96), 1) + 1)
            taps.append(dot(down, cols).astype(bf16))

        def window(first, factor=None):
            rows = []
            for kx in range(3):
                part = taps[0][first : first + 32, kx * width : (kx + 1) * width]
                if "tick" in pace and kx == 0:
                    part = paced(part.astype(f32)).astype(bf16)
                if factor is not None:
                    scale = jnp.where(iota((32, width), 0) == 0, factor, 1.0)
                    part = (part.astype(f32) * scale).astype(bf16)
                rows.append(part)
            return jnp.concatenate(rows + [blank], axis=0)

        def conv_first(first_row, lhs, *rhs):
            out = dot(w1t[lhs, :], jnp.concatenate([window(*w) for w in rhs], axis=1))
            for i in range(out.shape[0] // enc_ch):
                for j in range(len(rhs)):
                    feats[first_row + 8 * j + i] = out[
                        enc_ch * i : enc_ch * (i + 1), width * j : width * (j + 1)
                    ]

        def activate(r):
            v = feats[r]
            feats[r] = stack_cols(jnp.maximum(v, paced(v, SLOPE)), 2)

        def conv_second(p):
            x = jnp.concatenate([feats[2 * p], feats[2 * p + 1]], axis=1)
            if p == -5:
                parts[p] = (dot(w2c[:enc_ch, :], x), None, None)
            elif p == 12:
                parts[p] = (None, None, dot(w2c[2 * enc_ch :, :], x))
            else:
                t = dot(w2c[...], x)
                parts[p] = (t[:enc_ch], t[enc_ch : 2 * enc_ch], t[2 * enc_ch :])

        def wide(v, by):
            return jnp.concatenate([paced(v[:, :width], by), paced(v[:, width:], by)], axis=1)

        def project(o):
            before, mid, after = parts[o - 1][0], parts[o][1], parts[o + 1][2]
            before = wide(before, {0: low, 8: up}.get(o))
            after = wide(after, {-1: low, 7: up}.get(o))
            second = leaky(before + mid + after).astype(bf16)
            d = dot(w3_ref[...], second).astype(bf16).astype(f32)
            for half in range(2):
                row = 2 * o + half + 8
                dmap[pl.ds(row, desc_ch, stride=33), :] = d[:, half * width : (half + 1) * width]

        part = functools.partial
        steps = [start, part(conv_first, -10, slice(6 * enc_ch, None), (0,))]
        steps += [part(conv_first, -8 + i, slice(i * enc_ch, (i + 2) * enc_ch), (16,), (32, low)) for i in range(0, 8, 2)]
        steps += [part(conv_first, 8 + i, slice(i * enc_ch, (i + 2) * enc_ch), (48,), (64, up)) for i in range(0, 8, 2)]
        steps += [part(conv_first, 24, slice(0, 2 * enc_ch), (80,))]
        steps += [part(activate, r) for r in range(-10, 26)]
        for p in range(-5, 13):
            steps.append(part(conv_second, p))
            if p - LAG >= -4:
                steps.append(part(project, p - LAG))
        steps += [part(project, p) for p in range(13 - LAG, 12)]
        return steps

    def accumulate(state, dmap, sec_i, k, g, c):
        mine = [own[sec_i, 3 * g + b, c * 24 + 8 * k : c * 24 + 8 * k + 8, :] * one for b in range(3)]
        acc = state.get("acc")
        new = []
        for a in range(WINDOW):
            other = dmap[pl.ds(c * 33 + 8 * k + a, 8), :]
            for b in range(3):
                v = mine[b] * other
                new.append(v if acc is None else acc[3 * a + b] + v)
        state["acc"] = new
        if c % 8 == 7:
            pace["tick"] = new[0] * (1.0 - one) + one

    def put(cost, v, by, d, row):
        v = col_shift(v, by)
        last = WINDOW * WINDOW - 1
        for i, s in ((0, 0),) if d < last else ((0, -1), (1, 0), (2, 1)):
            moved = v if s == 0 else col_shift(v, s)
            cost[pl.ds(row * 97 + d + i, 8, stride=97), :] = moved

    def correlate(dmap, cost, sec_i, low_p, up_p, low_s, up_s):
        scale = 1.0 / math.sqrt(desc_ch)

        def finish(state, k, g, a):
            y = iota((8, width), 0) + (8 * k - RADIUS)
            yp = y + (a - RADIUS)
            mask = jnp.where(y < 0, low_s, jnp.where(y >= 16, up_s, 1.0)) * scale
            if k == 0:
                mask = jnp.where((y < 0) != (yp < 0), mask * low_p, mask)
            if k == 2:
                mask = jnp.where((y < 16) != (yp < 16), mask * up_p, mask)
            for b in range(3):
                v = state["acc"][3 * a + b] * (scale if k == 1 else mask)
                put(cost, v, 3 * g + b - RADIUS, a * WINDOW + 3 * g + b, 8 * k)

        part = functools.partial
        steps = []
        for k in range(3):
            for g in range(3):
                state = {}
                steps += [part(accumulate, state, dmap, sec_i, k, g, c) for c in range(desc_ch)]
                steps += [part(finish, state, k, g, a) for a in range(WINDOW)]
        return steps

    def decode(cost, sec_i, slot, low_s, up_s):
        t1, t2, t3 = {}, {}, {}

        def cost_row(row):
            at = (row + RADIUS) * 97
            v = paced(cost[at : at + 96, :]).astype(bf16)
            return jnp.concatenate([stack_cols(v[:80], 1), v[80:]], axis=0)

        def join(t, row, pitch, n):
            before, after = t[row - 1][:n], t[row + 1][2 * pitch : 2 * pitch + n]
            if n % 8:
                return before * one + t[row][pitch : pitch + n] + after * one
            return paced(before) + t[row][pitch : pitch + n] + paced(after)

        def hidden(t, row):
            v = leaky(join(t, row, enc_ch, enc_ch))
            if row < 0:
                v = v * low_s
            if row >= 16:
                v = v * up_s
            return stack_cols(v, 1)

        def multiply(t, weights, row, rows):
            out = dot(weights, jnp.concatenate(rows, axis=1))
            t[row], t[row + 1] = out[:, :width], out[:, width:]

        def first(p):
            multiply(t1, d1c[...], 2 * p, [cost_row(2 * p), cost_row(2 * p + 1)])

        def second(p):
            multiply(t2, d2c[...], 2 * p, [hidden(t1, 2 * p), hidden(t1, 2 * p + 1)])

        def third(p):
            rows = [hidden(t2, 2 * p - 1), hidden(t2, 2 * p)]
            multiply(t3, d3c[...].astype(bf16), 2 * p - 1, rows)
            for row in (2 * p - 2, 2 * p - 1):
                if 0 <= row < 16:
                    v = join(t3, row, 8, 2)
                    for o in range(2):
                        flow_ref[sec_i, slot, o, row : row + 1, :] = v[o : o + 1, :]

        part = functools.partial
        return (
            [part(first, p) for p in range(-2, 10)]
            + [part(second, p) for p in range(-1, 9)]
            + [part(third, p) for p in range(9)]
        )

    def run(*lists):
        keyed = [
            ((k + 0.5) / len(steps), n, k, f) for n, steps in enumerate(lists) for k, f in enumerate(steps)
        ]
        pace.clear()
        for _, _, _, f in sorted(keyed, key=lambda e: e[:3]):
            f()
        pace.clear()

    def section(sec_i, carry):
        mine = sec * here + sec_i
        run(encode(dmap_a, sec_i, link(mine, tile - 1), link(mine, tile)))

        def keep_own(c, carry):
            desc_ref[sec_i, c] = dmap_a[pl.ds(c * 33 + 8, 16), :].astype(bf16)
            for k in range(3):
                v = dmap_a[pl.ds(c * 33 + RADIUS + 8 * k, 8), :]
                at = pl.multiple_of(c * 24, 8) + 8 * k
                for b in range(WINDOW):
                    by = (b - RADIUS) % width
                    own[sec_i, b, pl.ds(at, 8), :] = pltpu.roll(v, by, axis=1) if by else v
            return carry

        return lax.fori_loop(0, desc_ch, keep_own, carry, unroll=4)

    lax.fori_loop(0, here, section, 0)

    n_slot = len(OFFSETS)
    n_pair = here * n_slot

    def pair_of(i):
        i = jnp.clip(i, 0, n_pair - 1)
        sec_i, slot = i // n_slot, i % n_slot
        mine = sec * here + sec_i
        other = partners_ref[sec_i, slot]
        dev = other // here
        near_a = (dev // 2) == ((sec // 2) ^ 1)
        block = jnp.where(dev // 2 == sec // 2, 0, jnp.where(near_a, 1, 2))
        twin = jnp.where(dev % 2 == sec % 2, 0, 1)
        cand = (block * 2 + twin) * here + other % here
        links = (link(other, tile - 1), link(other, tile), link(mine, tile - 1), link(mine, tile))
        return sec_i, slot, cand, links

    def encode_pair(i, dmap):
        _, _, cand, links = pair_of(i)
        return encode(dmap, cand, links[0], links[1])

    def decode_pair(i, cost):
        sec_i, slot, _, links = pair_of(i)
        return decode(cost, sec_i, slot, links[2], links[3])

    def phase(i, dmap, next_dmap, cost, last_cost):
        sec_i, _, _, links = pair_of(i)
        run(
            correlate(dmap, cost, sec_i, *links),
            decode_pair(i - 1, last_cost) + encode_pair(i + 1, next_dmap),
        )

    run(encode_pair(0, dmap_a))

    def two(k, carry):
        phase(2 * k, dmap_a, dmap_b, cost_a, cost_b)
        phase(2 * k + 1, dmap_b, dmap_a, cost_b, cost_a)
        return carry

    assert n_pair % 2 == 0
    lax.fori_loop(0, n_pair // 2, two, 0)
    run(decode_pair(n_pair - 1, cost_b))


def swap(x, axis, first, stride=1):
    size = lax.axis_size(axis)
    route = []
    for i in range(first * stride, size - stride):
        if (i // stride - first) % 2 == 0:
            route += [(i, i + stride), (i + stride, i)]
    return lax.ppermute(x, axis, route)


def shards(
    images, seam_links, partners, enc_first, enc_second, enc_third, dec_first, dec_second, dec_third
):
    here, height, in_width = images.shape
    assert here * 2 >= max(OFFSETS) and lax.axis_size("sec") % 2 == 0
    meta = jnp.stack([lax.axis_index("sec"), lax.axis_index("tile")]).astype(jnp.int32)
    near = jnp.concatenate([images, swap(images, "sec", 0)], axis=0)
    cands = jnp.concatenate([near, swap(near, "sec", 0, 2), swap(near, "sec", 1, 2)], axis=0)
    ha = swap(cands, "tile", 0)
    hb = swap(cands, "tile", 1)

    def taps(w):
        return jnp.transpose(w, (2, 3, 0, 1)).reshape((-1,) + w.shape[:2])

    w1 = jnp.transpose(enc_first, (1, 2, 3, 0)).reshape(9, -1)
    w3 = enc_third[:, :, 0, 0]
    enc_ch = enc_first.shape[0]
    desc_ch = enc_third.shape[0]
    rows, width = height // 2, in_width // 2
    smem = pl.BlockSpec(memory_space=pltpu.SMEM)
    vmem = pl.BlockSpec(memory_space=pltpu.VMEM)
    return pl.pallas_call(
        body,
        in_specs=[smem] * 3 + [vmem] * 9,
        out_specs=[vmem] * 2,
        out_shape=[
            jax.ShapeDtypeStruct((here, desc_ch, rows, width), bf16),
            jax.ShapeDtypeStruct((here, len(OFFSETS), dec_third.shape[0], rows, width), f32),
        ],
        scratch_shapes=[
            pltpu.VMEM((in_width, 3 * width), bf16),
            pltpu.VMEM((8 * enc_ch, 128), bf16),
            pltpu.VMEM((3 * enc_ch, 3 * enc_ch), bf16),
            pltpu.VMEM((3 * enc_ch, 256), bf16),
            pltpu.VMEM((3 * enc_ch, 3 * enc_ch), bf16),
            pltpu.VMEM((24, 3 * enc_ch), f32),
            pltpu.VMEM((desc_ch * 33, width), f32),
            pltpu.VMEM((desc_ch * 33, width), f32),
            pltpu.VMEM((here, WINDOW, desc_ch * 24, width), f32),
            pltpu.VMEM((24 * 97, width), f32),
            pltpu.VMEM((24 * 97, width), f32),
        ],
        compiler_params=pltpu.CompilerParams(vmem_limit_bytes=48 * 1024 * 1024),
    )(meta, seam_links, partners, cands, ha, hb, w1, taps(enc_second), w3, taps(dec_first),
      taps(dec_second), taps(dec_third))


def solution(mesh):
    return jax.shard_map(
        shards,
        mesh=mesh,
        in_specs=(P("sec", "tile", None), P(), P("sec", None), P(), P(), P(), P(), P(), P()),
        out_specs=(P("sec", None, "tile", None), P("sec", None, None, "tile", None)),
        check_vma=False,
    )
```

```python
import functools
import math

import jax
import jax.numpy as jnp
from jax import lax
from jax.experimental import pallas as pl
from jax.experimental.pallas import tpu as pltpu
from jax.sharding import PartitionSpec as P

RADIUS = 4
WINDOW = 2 * RADIUS + 1
SLOPE = 0.1
LAG = 3
OFFSETS = (1, 2, 4)

f32 = jnp.float32
bf16 = jnp.bfloat16


def dot(a, b):
    return jnp.dot(a, b, preferred_element_type=f32)


def leaky(v):
    return jnp.maximum(v, SLOPE * v)


def iota(shape, dim):
    return lax.broadcasted_iota(jnp.int32, shape, dim)


def col_shift(v, by):
    width = v.shape[-1]
    rolled = pltpu.roll(v, (-by) % width, axis=v.ndim - 1)
    x = iota(v.shape, v.ndim - 1) + by
    return jnp.where((x >= 0) & (x < width), rolled, jnp.zeros_like(rolled))


def stack_cols(v, by):
    v = v.astype(bf16)
    return jnp.concatenate([col_shift(v, -by), v, col_shift(v, by)], axis=0)


def onehot(shape, cond):
    return jnp.where(cond, 1.0, 0.0).astype(bf16)


def body(
    meta_ref, links_ref, partners_ref, img_ref, ha_ref, hb_ref,
    w1_ref, w2_ref, w3_ref, d1_ref, d2_ref, d3_ref,
    desc_ref, flow_ref,
    sel, w1t, w2c, d1c, d2c, d3c, dmap_a, dmap_b, own, cost_a, cost_b,
):
    here = img_ref.shape[0] // 6
    n_seam = links_ref.shape[1]
    sec = meta_ref[0]
    tile = meta_ref[1]
    desc_ch = w3_ref.shape[0]
    enc_ch = w3_ref.shape[1]
    width = desc_ref.shape[3]
    in_width = img_ref.shape[2]

    r = iota((in_width, 3 * width), 0)
    q = iota((in_width, 3 * width), 1)
    sel[...] = onehot(None, r == 2 * (q % width) + q // width - 1)
    j = iota((9, 8 * 128), 0)
    lane = iota((9, 8 * 128), 1)
    m, kx, ql = lane // 128, (lane % 128) // 32, lane % 32
    place = onehot(None, (j % 3 == kx) & (ql == 2 * m + j // 3))
    spread = lax.dot_general(
        w1_ref[...], place, (((0,), (0,)), ((), ())), preferred_element_type=f32
    ).astype(bf16)
    for i in range(8):
        w1t[enc_ch * i : enc_ch * (i + 1), :] = spread[:, 128 * i : 128 * (i + 1)]
    disp = d1_ref.shape[2]
    main = disp - 1
    r = iota((disp, 256), 0)
    q = iota((disp, 256), 1)
    for ky in range(3):
        acc = jnp.zeros((enc_ch, 256), f32)
        for kx in range(3):
            put = onehot(None, ((r < main) & (q == kx * main + r)) | ((r == main) & (q == 3 * main + kx)))
            acc = acc + dot(d1_ref[3 * ky + kx], put)
        d1c[enc_ch * ky : enc_ch * (ky + 1), :] = acc.astype(bf16)
        r2 = iota((enc_ch, 3 * enc_ch), 0)
        q2 = iota((enc_ch, 3 * enc_ch), 1)
        for src, dst, pitch in ((w2_ref, w2c, enc_ch), (d2_ref, d2c, enc_ch), (d3_ref, d3c, 8)):
            rows = src.shape[1]
            acc = jnp.zeros((rows, 3 * enc_ch), f32)
            for kx in range(3):
                acc = acc + dot(src[3 * ky + kx], onehot(None, q2 == kx * enc_ch + r2))
            dst[pitch * ky : pitch * ky + rows, :] = acc.astype(dst.dtype)
    for cost in (cost_a, cost_b):
        cost[...] = jnp.zeros_like(cost)
    even = tile % 2 == 0
    one = jnp.where(tile >= 0, 1.0, 0.0).astype(f32)
    pace = {}

    def paced(v, by=None):
        tick = pace.get("tick")
        if tick is None:
            return v * (one if by is None else by)
        factor = tick if by is None else tick * by
        return (v.reshape(-1, 8, width) * factor[None]).reshape(v.shape)


    def link(section, seam):
        inside = (seam >= 0) & (seam < n_seam)
        value = links_ref[section, jnp.clip(seam, 0, n_seam - 1)]
        return jnp.where(inside, value, 0).astype(f32)

    def encode(dmap, cand, low, up):
        taps, feats, parts = [], {}, {}
        blank = jnp.zeros((32, width), bf16)

        def start():
            first, second = ha_ref[cand], hb_ref[cand]
            strip = [jnp.where(even, second, first), img_ref[cand], jnp.where(even, first, second)]
            cols = dot(jnp.concatenate(strip, axis=0), sel[...]).astype(bf16)
            down = onehot(None, iota((112, 96), 0) == iota((112, 96), 1) + 1)
            taps.append(dot(down, cols).astype(bf16))

        def window(first, factor=None):
            rows = []
            for kx in range(3):
                part = taps[0][first : first + 32, kx * width : (kx + 1) * width]
                if "tick" in pace and kx == 0:
                    part = paced(part.astype(f32)).astype(bf16)
                if factor is not None:
                    scale = jnp.where(iota((32, width), 0) == 0, factor, 1.0)
                    part = (part.astype(f32) * scale).astype(bf16)
                rows.append(part)
            return jnp.concatenate(rows + [blank], axis=0)

        def conv_first(first_row, lhs, *rhs):
            out = dot(w1t[lhs, :], jnp.concatenate([window(*w) for w in rhs], axis=1))
            for i in range(out.shape[0] // enc_ch):
                for j in range(len(rhs)):
                    feats[first_row + 8 * j + i] = out[
                        enc_ch * i : enc_ch * (i + 1), width * j : width * (j + 1)
                    ]

        def activate(r):
            v = feats[r]
            feats[r] = stack_cols(jnp.maximum(v, paced(v, SLOPE)), 2)

        def conv_second(p):
            x = jnp.concatenate([feats[2 * p], feats[2 * p + 1]], axis=1)
            if p == -5:
                parts[p] = (dot(w2c[:enc_ch, :], x), None, None)
            elif p == 12:
                parts[p] = (None, None, dot(w2c[2 * enc_ch :, :], x))
            else:
                t = dot(w2c[...], x)
                parts[p] = (t[:enc_ch], t[enc_ch : 2 * enc_ch], t[2 * enc_ch :])

        def wide(v, by):
            return jnp.concatenate([paced(v[:, :width], by), paced(v[:, width:], by)], axis=1)

        def project(o):
            before, mid, after = parts[o - 1][0], parts[o][1], parts[o + 1][2]
            before = wide(before, {0: low, 8: up}.get(o))
            after = wide(after, {-1: low, 7: up}.get(o))
            second = leaky(before + mid + after).astype(bf16)
            d = dot(w3_ref[...], second).astype(bf16).astype(f32)
            for half in range(2):
                row = 2 * o + half + 8
                dmap[pl.ds(row, desc_ch, stride=33), :] = d[:, half * width : (half + 1) * width]

        part = functools.partial
        steps = [start, part(conv_first, -10, slice(6 * enc_ch, None), (0,))]
        steps += [part(conv_first, -8 + i, slice(i * enc_ch, (i + 2) * enc_ch), (16,), (32, low)) for i in range(0, 8, 2)]
        steps += [part(conv_first, 8 + i, slice(i * enc_ch, (i + 2) * enc_ch), (48,), (64, up)) for i in range(0, 8, 2)]
        steps += [part(conv_first, 24, slice(0, 2 * enc_ch), (80,))]
        steps += [part(activate, r) for r in range(-10, 26)]
        for p in range(-5, 13):
            steps.append(part(conv_second, p))
            if p - LAG >= -4:
                steps.append(part(project, p - LAG))
        steps += [part(project, p) for p in range(13 - LAG, 12)]
        return steps

    def accumulate(state, dmap, sec_i, k, b0, n, c):
        mine = [own[sec_i, b0 + b, c * 24 + 8 * k : c * 24 + 8 * k + 8, :] * one for b in range(n)]
        acc = state.get("acc")
        new = []
        for a in range(WINDOW):
            other = dmap[pl.ds(c * 33 + 8 * k + a, 8), :]
            for b in range(n):
                v = mine[b] * other
                new.append(v if acc is None else acc[n * a + b] + v)
        state["acc"] = new
        if c % 16 == 15:
            pace["tick"] = new[0] * (1.0 - one) + one

    def put(cost, v, by, d, row):
        v = col_shift(v, by)
        last = WINDOW * WINDOW - 1
        for i, s in ((0, 0),) if d < last else ((0, -1), (1, 0), (2, 1)):
            moved = v if s == 0 else col_shift(v, s)
            cost[pl.ds(row * 97 + d + i, 8, stride=97), :] = moved

    def correlate(dmap, cost, sec_i, low_p, up_p, low_s, up_s):
        scale = 1.0 / math.sqrt(desc_ch)

        def finish(state, k, b0, n, a):
            y = iota((8, width), 0) + (8 * k - RADIUS)
            yp = y + (a - RADIUS)
            mask = jnp.where(y < 0, low_s, jnp.where(y >= 16, up_s, 1.0)) * scale
            if k == 0:
                mask = jnp.where((y < 0) != (yp < 0), mask * low_p, mask)
            if k == 2:
                mask = jnp.where((y < 16) != (yp < 16), mask * up_p, mask)
            for b in range(n):
                v = state["acc"][n * a + b] * (scale if k == 1 else mask)
                put(cost, v, b0 + b - RADIUS, a * WINDOW + b0 + b, 8 * k)

        part = functools.partial
        steps = []
        for k in range(3):
            for b0 in range(WINDOW):
                n = 1
                state = {}
                steps += [part(accumulate, state, dmap, sec_i, k, b0, n, c) for c in range(desc_ch)]
                steps += [part(finish, state, k, b0, n, a) for a in range(WINDOW)]
        return steps

    def decode(cost, sec_i, slot, low_s, up_s):
        t1, t2, t3 = {}, {}, {}

        def cost_row(row):
            at = (row + RADIUS) * 97
            v = paced(cost[at : at + 96, :]).astype(bf16)
            return jnp.concatenate([stack_cols(v[:80], 1), v[80:]], axis=0)

        def join(t, row, pitch, n):
            before, after = t[row - 1][:n], t[row + 1][2 * pitch : 2 * pitch + n]
            if n % 8:
                return before * one + t[row][pitch : pitch + n] + after * one
            return paced(before) + t[row][pitch : pitch + n] + paced(after)

        def hidden(t, row):
            v = leaky(join(t, row, enc_ch, enc_ch))
            if row < 0:
                v = v * low_s
            if row >= 16:
                v = v * up_s
            return stack_cols(v, 1)

        def multiply(t, weights, row, rows):
            out = dot(weights, jnp.concatenate(rows, axis=1))
            t[row], t[row + 1] = out[:, :width], out[:, width:]

        def first(p):
            multiply(t1, d1c[...], 2 * p, [cost_row(2 * p), cost_row(2 * p + 1)])

        def second(p):
            multiply(t2, d2c[...], 2 * p, [hidden(t1, 2 * p), hidden(t1, 2 * p + 1)])

        def third(p):
            rows = [hidden(t2, 2 * p - 1), hidden(t2, 2 * p)]
            multiply(t3, d3c[...].astype(bf16), 2 * p - 1, rows)
            for row in (2 * p - 2, 2 * p - 1):
                if 0 <= row < 16:
                    v = join(t3, row, 8, 2)
                    for o in range(2):
                        flow_ref[sec_i, slot, o, row : row + 1, :] = v[o : o + 1, :]

        part = functools.partial
        return (
            [part(first, p) for p in range(-2, 10)]
            + [part(second, p) for p in range(-1, 9)]
            + [part(third, p) for p in range(9)]
        )

    def run(*lists):
        keyed = [
            ((k + 0.5) / len(steps), n, k, f) for n, steps in enumerate(lists) for k, f in enumerate(steps)
        ]
        pace.clear()
        for _, _, _, f in sorted(keyed, key=lambda e: e[:3]):
            f()
        pace.clear()

    def section(sec_i, carry):
        mine = sec * here + sec_i
        run(encode(dmap_a, sec_i, link(mine, tile - 1), link(mine, tile)))

        def keep_own(c, carry):
            desc_ref[sec_i, c] = dmap_a[pl.ds(c * 33 + 8, 16), :].astype(bf16)
            for k in range(3):
                v = dmap_a[pl.ds(c * 33 + RADIUS + 8 * k, 8), :]
                at = pl.multiple_of(c * 24, 8) + 8 * k
                for b in range(WINDOW):
                    by = (b - RADIUS) % width
                    own[sec_i, b, pl.ds(at, 8), :] = pltpu.roll(v, by, axis=1) if by else v
            return carry

        return lax.fori_loop(0, desc_ch, keep_own, carry, unroll=8)

    lax.fori_loop(0, here, section, 0)

    n_slot = len(OFFSETS)
    n_pair = here * n_slot

    def pair_of(i):
        i = jnp.clip(i, 0, n_pair - 1)
        sec_i, slot = i // n_slot, i % n_slot
        mine = sec * here + sec_i
        other = partners_ref[sec_i, slot]
        dev = other // here
        near_a = (dev // 2) == ((sec // 2) ^ 1)
        block = jnp.where(dev // 2 == sec // 2, 0, jnp.where(near_a, 1, 2))
        twin = jnp.where(dev % 2 == sec % 2, 0, 1)
        cand = (block * 2 + twin) * here + other % here
        links = (link(other, tile - 1), link(other, tile), link(mine, tile - 1), link(mine, tile))
        return sec_i, slot, cand, links

    def encode_pair(i, dmap):
        _, _, cand, links = pair_of(i)
        return encode(dmap, cand, links[0], links[1])

    def decode_pair(i, cost):
        sec_i, slot, _, links = pair_of(i)
        return decode(cost, sec_i, slot, links[2], links[3])

    def phase(i, dmap, next_dmap, cost, last_cost):
        sec_i, _, _, links = pair_of(i)
        run(
            correlate(dmap, cost, sec_i, *links),
            decode_pair(i - 1, last_cost) + encode_pair(i + 1, next_dmap),
        )

    run(encode_pair(0, dmap_a))

    def two(k, carry):
        phase(2 * k, dmap_a, dmap_b, cost_a, cost_b)
        phase(2 * k + 1, dmap_b, dmap_a, cost_b, cost_a)
        return carry

    assert n_pair % 2 == 0
    lax.fori_loop(0, n_pair // 2, two, 0)
    run(decode_pair(n_pair - 1, cost_b))


def swap(x, axis, first, stride=1):
    size = lax.axis_size(axis)
    route = []
    for i in range(first * stride, size - stride):
        if (i // stride - first) % 2 == 0:
            route += [(i, i + stride), (i + stride, i)]
    return lax.ppermute(x, axis, route)


def shards(
    images, seam_links, partners, enc_first, enc_second, enc_third, dec_first, dec_second, dec_third
):
    here, height, in_width = images.shape
    assert here * 2 >= max(OFFSETS) and lax.axis_size("sec") % 2 == 0
    meta = jnp.stack([lax.axis_index("sec"), lax.axis_index("tile")]).astype(jnp.int32)
    near = jnp.concatenate([images, swap(images, "sec", 0)], axis=0)
    cands = jnp.concatenate([near, swap(near, "sec", 0, 2), swap(near, "sec", 1, 2)], axis=0)
    ha = swap(cands, "tile", 0)
    hb = swap(cands, "tile", 1)

    def taps(w):
        return jnp.transpose(w, (2, 3, 0, 1)).reshape((-1,) + w.shape[:2])

    w1 = jnp.transpose(enc_first, (1, 2, 3, 0)).reshape(9, -1)
    w3 = enc_third[:, :, 0, 0]
    enc_ch = enc_first.shape[0]
    desc_ch = enc_third.shape[0]
    rows, width = height // 2, in_width // 2
    smem = pl.BlockSpec(memory_space=pltpu.SMEM)
    vmem = pl.BlockSpec(memory_space=pltpu.VMEM)
    return pl.pallas_call(
        body,
        in_specs=[smem] * 3 + [vmem] * 9,
        out_specs=[vmem] * 2,
        out_shape=[
            jax.ShapeDtypeStruct((here, desc_ch, rows, width), bf16),
            jax.ShapeDtypeStruct((here, len(OFFSETS), dec_third.shape[0], rows, width), f32),
        ],
        scratch_shapes=[
            pltpu.VMEM((in_width, 3 * width), bf16),
            pltpu.VMEM((8 * enc_ch, 128), bf16),
            pltpu.VMEM((3 * enc_ch, 3 * enc_ch), bf16),
            pltpu.VMEM((3 * enc_ch, 256), bf16),
            pltpu.VMEM((3 * enc_ch, 3 * enc_ch), bf16),
            pltpu.VMEM((24, 3 * enc_ch), f32),
            pltpu.VMEM((desc_ch * 33, width), f32),
            pltpu.VMEM((desc_ch * 33, width), f32),
            pltpu.VMEM((here, WINDOW, desc_ch * 24, width), f32),
            pltpu.VMEM((24 * 97, width), f32),
            pltpu.VMEM((24 * 97, width), f32),
        ],
        compiler_params=pltpu.CompilerParams(vmem_limit_bytes=48 * 1024 * 1024),
    )(meta, seam_links, partners, cands, ha, hb, w1, taps(enc_second), w3, taps(dec_first),
      taps(dec_second), taps(dec_third))


def solution(mesh):
    return jax.shard_map(
        shards,
        mesh=mesh,
        in_specs=(P("sec", "tile", None), P(), P("sec", None), P(), P(), P(), P(), P(), P()),
        out_specs=(P("sec", None, "tile", None), P("sec", None, None, "tile", None)),
        check_vma=False,
    )
```
